32 devices in a mesh: smp: 2 (over x), proto: 16 (over z, y, core).
Axes of the slice: x: 2, y: 2, z: 4, core: 2. Of those that a mesh axis runs over, the one named last changes fastest.
Arguments:
- teacher_features: bfloat16 [256, 512], P('smp', 'proto'), may hold values from -6 to 6
- student_features: bfloat16 [256, 512], P('smp', 'proto'), may hold values from -6 to 6
- teacher_weight: bfloat16 [131072, 512], P('proto'), may hold values from -0.45 to 0.45
- student_weight: bfloat16 [131072, 512], P('proto'), may hold values from -0.19921875 to 0.19921875
Outputs:
- sample_loss: float32 [256], P('smp')
- grad_features: float32 [256, 512], P('smp', 'proto')
- grad_weight: float32 [131072, 512], P('proto', 'smp')
The draws below stay inside these ranges and needn't reach their ends.
All inputs are finite; a program needn't handle non-finite values.
Results may differ from the reference program's by a relative error of at most 0.0085.
Values may be sent and summed in bfloat16 or wider, within the bound.
A program may use at most 64 MiB of HBM per device.

```python
import math
import jax
import jax.numpy as jnp
from jax import lax

D = 512
K = 131072
B_DEV = 128
ITERS = 3
B = 256
N_SMP = 2


cluster_count = 4


center_gain = 0.3


noise_level = 0.07


student_gain = 0.15


student_noise = 0.05


student_bound = 0.19921875


def cluster_centers(key):
    raw = jax.random.normal(jax.random.fold_in(key, 7101), (cluster_count, D), jnp.float32)
    return raw / jnp.sqrt(jnp.sum(raw * raw, axis=1, keepdims=True))


def spread_centers(labels, centers):
    onehot = (labels[:, None] == jnp.arange(cluster_count, dtype=jnp.int32)[None, :]).astype(jnp.float32)
    return jnp.dot(onehot, centers, precision=lax.Precision.HIGHEST)


def sample_labels(key):
    blocks = B // B_DEV
    dominant = jax.random.randint(jax.random.fold_in(key, 7707), (blocks,), 0, cluster_count).astype(jnp.int32)
    ticket = jax.random.randint(jax.random.fold_in(key, 7202), (B,), 0, 20).astype(jnp.int32)
    offset = jax.random.randint(jax.random.fold_in(key, 7808), (B,), 1, cluster_count).astype(jnp.int32)
    block_of = jnp.arange(B, dtype=jnp.int32) // B_DEV
    leader = dominant[block_of]
    return jnp.where(ticket < 15, leader, (leader + offset) % cluster_count).astype(jnp.int32)


def prototype_labels(key):
    ticket = jax.random.randint(jax.random.fold_in(key, 7505), (K,), 0, 10).astype(jnp.int32)
    return (ticket >= 1).astype(jnp.int32) + (ticket >= 3).astype(jnp.int32) + (ticket >= 6).astype(jnp.int32)


def feature_rows(key, noise_fold):
    centers = cluster_centers(key)
    anchor = spread_centers(sample_labels(key), centers) * math.sqrt(D)
    noise_key = jax.random.fold_in(key, noise_fold)
    noise = jnp.clip(jax.random.normal(noise_key, (B, D), jnp.float32), -4.0, 4.0)
    mixed = math.sqrt(0.5) * anchor + math.sqrt(0.5) * noise
    return jnp.clip(mixed, -6.0, 6.0)


def draw_teacher_features(key, part):
    return feature_rows(key, 7303).astype(jnp.bfloat16)


def draw_student_features(key, part):
    return feature_rows(key, 8101).astype(jnp.bfloat16)


def draw_teacher_weight(key, part):
    centers = cluster_centers(key)
    anchor = spread_centers(prototype_labels(key), centers) * center_gain
    noise_key = jax.random.fold_in(key, 7606)
    noise = jnp.clip(noise_level * jax.random.normal(noise_key, (K, D), jnp.float32), -0.3, 0.3)
    return jnp.clip(anchor + noise, -0.45, 0.45).astype(jnp.bfloat16)


def draw_student_weight(key, part):
    centers = cluster_centers(key)
    anchor = spread_centers(prototype_labels(key), centers) * student_gain
    noise_key = jax.random.fold_in(key, 8303)
    noise = jnp.clip(student_noise * jax.random.normal(noise_key, (K, D), jnp.float32), -0.18, 0.18)
    return jnp.clip(anchor + noise, -student_bound, student_bound).astype(jnp.bfloat16)


def setup_inputs(seed: int = 0) -> dict:
    keys = jax.random.split(jax.random.key(seed), 5)
    return {
        "teacher_features": draw_teacher_features(jax.random.fold_in(keys[4], 71), 0),
        "student_features": draw_student_features(jax.random.fold_in(keys[4], 71), 0),
        "teacher_weight": draw_teacher_weight(jax.random.fold_in(keys[4], 71), 0),
        "student_weight": draw_student_weight(jax.random.fold_in(keys[4], 71), 0),
    }


TEACHER_TEMP = 0.07
STUDENT_TEMP = 0.1

def unit_rows(features):
    values = features.astype(jnp.float32)
    scale = lax.rsqrt(lax.optimization_barrier(jnp.sum(values * values, axis=1)) + 1e-06)
    return ((values * scale[:, None]).astype(jnp.bfloat16), scale)

def project(rows, weight):
    return lax.dot_general(rows, weight, (((1,), (1,)), ((), ())), preferred_element_type=jnp.float32)

def reference(teacher_features, student_features, teacher_weight, student_weight):
    samples = teacher_features.shape[0]
    protos = teacher_weight.shape[0]
    teacher_unit, unused = unit_rows(teacher_features)
    student_unit, student_scale = unit_rows(student_features)
    kernel = jnp.exp(project(teacher_unit, teacher_weight) / TEACHER_TEMP)
    col_scale = jnp.ones((samples,), jnp.float32)
    row_scale = jnp.ones((protos,), jnp.float32)
    for step in range(ITERS):
        row_scale = 1.0 / (protos * jnp.dot(col_scale, kernel, precision=lax.Precision.HIGHEST))
        col_scale = 1.0 / (samples * jnp.dot(kernel, row_scale, precision=lax.Precision.HIGHEST))
    block_rows = samples // N_SMP

    def one_block(weight_total, block_index):
        start = (block_index * block_rows).astype(jnp.int32)
        kernel_block = lax.dynamic_slice_in_dim(kernel, start, block_rows, 0)
        unit_block = lax.dynamic_slice_in_dim(student_unit, start, block_rows, 0)
        scale_block = lax.dynamic_slice_in_dim(student_scale, start, block_rows, 0)
        col_block = lax.dynamic_slice_in_dim(col_scale, start, block_rows, 0)
        feats = lax.dynamic_slice_in_dim(student_features, start, block_rows, 0).astype(jnp.float32)
        targets = samples * kernel_block * row_scale[None, :] * col_block[:, None]
        logits = project(unit_block, student_weight) / STUDENT_TEMP
        expo = jnp.exp(logits)
        totals = lax.optimization_barrier(jnp.sum(expo, axis=1))
        weighted = lax.optimization_barrier(jnp.sum(targets * logits, axis=1))
        probs = expo / totals[:, None]
        loss_block = jnp.log(totals) - weighted
        logit_grad = ((probs - targets) / (samples * STUDENT_TEMP)).astype(jnp.bfloat16)
        unit_grad = jnp.dot(logit_grad, student_weight, preferred_element_type=jnp.float32)
        inner_prod = lax.optimization_barrier(jnp.sum(feats * unit_grad, axis=1))
        grad_block = scale_block[:, None] * unit_grad - (scale_block ** 3 * inner_prod)[:, None] * feats
        weight_part = lax.dot_general(logit_grad, unit_block, (((0,), (0,)), ((), ())), preferred_element_type=jnp.float32)
        weight_total = weight_total + weight_part.astype(jnp.bfloat16).astype(jnp.float32)
        return (weight_total, (loss_block, grad_block))
    start_carry = jnp.zeros(student_weight.shape, jnp.float32)
    grad_weight, (loss_blocks, grad_blocks) = lax.scan(one_block, start_carry, jnp.arange(N_SMP, dtype=jnp.int32))
    grad_features = grad_blocks.reshape(student_features.shape)
    return (loss_blocks.reshape((samples,)), grad_features, grad_weight)
```

```python
import functools

import jax
import jax.numpy as jnp
from jax import lax
from jax.experimental import pallas as pl
from jax.experimental.pallas import tpu as pltpu
from jax.sharding import PartitionSpec as P

TEACHER_TEMP = 0.07
STUDENT_TEMP = 0.1
MESH = pl.DeviceIdType.MESH
F32 = jnp.float32
BF16 = jnp.bfloat16


def loop(count, body):
    if count <= 16:
        for i in range(count):
            body(i)
    else:
        lax.fori_loop(0, count, lambda i, c: (body(i), c)[1], 0)


def fold(x):
    return jnp.sum(x.reshape(x.shape[0] // 8, 8, x.shape[1]), axis=0)


def kernel(
    n_smp, n_proto, iters, kb,
    feat_ref, wt_hbm, ws_hbm,
    loss_ref, gfeat_ref, gw_hbm,
    fbuf, wt, ws, kern, logit, expo, gw, ut, us, lgbuf, sscale, rowbuf, stage,
    ubuf, ibuf, usend, isend,
    wt_sem, ws_sem, gw_sem, own_sem, fs_proto, fs_smp, fs_core, fr,
    ar_send, ar_recv, u_send, u_recv, i_send, i_recv,
):
    s = lax.axis_index("smp")
    p = lax.axis_index("proto")
    protos_local, depth = wt.shape
    rows2, lanes = feat_ref.shape
    rows = rows2 // 2
    samples = n_smp * lanes
    protos = n_proto * protos_local
    blocks = protos_local // kb
    pairs = n_proto // 2
    core = p % 2
    pair = p // 2
    mate = pair * 2 + (1 - core)
    width = gw.shape[1]

    def wcopy(hbm, vmem, sem, i):
        part = pl.ds(i * kb, kb)
        return pltpu.make_async_copy(hbm.at[part], vmem.at[part], sem.at[i])

    own = pltpu.make_async_copy(feat_ref, fbuf.at[s, p], own_sem)
    own.start()
    loop(blocks, lambda i: wcopy(wt_hbm, wt, wt_sem, i).start())
    loop(blocks, lambda i: wcopy(ws_hbm, ws, ws_sem, i).start())

    barrier = pltpu.get_barrier_semaphore()

    def greet_proto(i):
        pl.semaphore_signal(barrier, inc=1, device_id=(s, (p + 1 + i) % n_proto), device_id_type=MESH)

    def greet_smp(i):
        pl.semaphore_signal(barrier, inc=1, device_id=((s + 1 + i) % n_smp, p), device_id_type=MESH)

    loop(n_proto - 1, greet_proto)
    loop(n_smp - 1, greet_smp)
    pl.semaphore_wait(barrier, n_proto + n_smp - 2)

    own.wait()

    def chunk(cs, cp, send_sem, target):
        slot = fbuf.at[cs, cp]
        return pltpu.make_async_remote_copy(
            src_ref=slot, dst_ref=slot, send_sem=send_sem, recv_sem=fr.at[cs, cp],
            device_id=target, device_id_type=MESH,
        )

    def peer(i):
        return ((pair + i) % pairs) * 2 + core

    def to_proto(i):
        return chunk(s, p, fs_proto.at[i], (s, peer(i + 1)))

    def to_smp(i, j):
        return chunk(s, peer(i), fs_smp.at[i, j], ((s + 1 + j) % n_smp, p))

    def to_core(j, i):
        return chunk((s + j) % n_smp, peer(i), fs_core.at[j, i], (s, mate))

    def arrived(cs, cp):
        chunk(cs, cp, own_sem, (s, mate)).wait_recv()

    loop(n_smp - 1, lambda j: to_smp(0, j).start())
    loop(pairs - 1, lambda i: to_proto(i).start())
    to_core(0, 0).start()

    def relay_proto(i):
        arrived(s, peer(i + 1))
        loop(n_smp - 1, lambda j: to_smp(i + 1, j).start())
        to_core(0, i + 1).start()

    loop(pairs - 1, relay_proto)

    def relay_smp(m):
        j = 1 + m // pairs
        i = m % pairs
        arrived((s + j) % n_smp, peer(i))
        to_core(j, i).start()

    loop((n_smp - 1) * pairs, relay_smp)

    def from_core(m):
        arrived((s + m // pairs) % n_smp, ((pair + m % pairs) % pairs) * 2 + 1 - core)

    loop(n_smp * pairs, from_core)

    def halves(x):
        x = x.astype(F32)
        return x[:, :rows].reshape(depth, lanes), x[:, rows:].reshape(depth, lanes)

    for q in range(n_smp):
        teach, stud = halves(fbuf[q])
        here = slice(q * lanes, (q + 1) * lanes)
        t_scale = lax.rsqrt(jnp.sum(teach * teach, axis=0, keepdims=True) + 1e-06)
        s_scale = lax.rsqrt(jnp.sum(stud * stud, axis=0, keepdims=True) + 1e-06)
        ut[:, here] = (teach * t_scale).astype(BF16)
        us[:, here] = (stud * s_scale).astype(BF16)
        sscale[:, here] = s_scale

    def share(r):
        def one(i):
            slot = rowbuf.at[r, p]
            return pltpu.make_async_remote_copy(
                src_ref=slot, dst_ref=slot, send_sem=ar_send.at[r, i], recv_sem=ar_recv.at[r, p],
                device_id=(s, (p + 1 + i) % n_proto), device_id_type=MESH,
            )
        return one

    def gathered(r):
        def one(i):
            q = (p + 1 + i) % n_proto
            slot = rowbuf.at[r, q]
            pltpu.make_async_remote_copy(
                src_ref=slot, dst_ref=slot, send_sem=ar_send.at[r, i], recv_sem=ar_recv.at[r, q],
                device_id=(s, q), device_id_type=MESH,
            ).wait_recv()
        loop(n_proto - 1, one)
        return jnp.sum(rowbuf[r], axis=0)

    def put(r, first, second):
        rowbuf[r, p, 0:1, :] = jnp.sum(first, axis=0, keepdims=True)
        rowbuf[r, p, 1:2, :] = jnp.sum(second, axis=0, keepdims=True)
        loop(n_proto - 1, lambda i: share(r)(i).start())

    zero = jnp.zeros((8, samples), F32)

    def teacher_block(i, acc):
        wcopy(wt_hbm, wt, wt_sem, i).wait()
        part = pl.ds(pl.multiple_of(i * kb, kb), kb)
        value = jnp.exp(jnp.dot(wt[part, :], ut[...], preferred_element_type=F32) * (1.0 / TEACHER_TEMP))
        kern[part, :] = value
        row = 1.0 / (protos * jnp.sum(value, axis=1, keepdims=True))
        return acc + fold(value * row)

    def student_block(i, acc):
        wcopy(ws_hbm, ws, ws_sem, i).wait()
        part = pl.ds(pl.multiple_of(i * kb, kb), kb)
        value = jnp.dot(ws[part, :], us[...], preferred_element_type=F32) * (1.0 / STUDENT_TEMP)
        logit[part, :] = value
        value = jnp.exp(value)
        expo[part, :] = value
        return acc + fold(value)

    put(0, lax.fori_loop(0, blocks, teacher_block, zero), zero)
    exp_part = lax.fori_loop(0, blocks, student_block, zero)
    exp_total = None
    for step in range(1, iters):
        total = gathered(step - 1)
        if step == 2:
            exp_total = total[1:2]
        col = 1.0 / (samples * total[0:1])
        last = step == iters - 1

        def pass_block(i, acc, col=col, last=last):
            part = pl.ds(pl.multiple_of(i * kb, kb), kb)
            value = kern[part, :]
            row = 1.0 / (protos * jnp.sum(value * col, axis=1, keepdims=True))
            value = value * row
            if not last:
                return (acc[0] + fold(value),)
            kern[part, :] = value
            return (acc[0] + fold(value), acc[1] + fold(value * logit[part, :]))

        if last:
            first, second = lax.fori_loop(0, blocks, pass_block, (zero, zero))
        else:
            first, second = lax.fori_loop(0, blocks, pass_block, (zero,))[0], exp_part
        put(step, first, second)

    total = gathered(iters - 1)
    target_scale = samples * (1.0 / (samples * total[0:1]))
    stage[...] = jnp.log(exp_total) - target_scale * total[1:2]
    loss_ref[...] = stage[:, pl.ds(pl.multiple_of(s * lanes, lanes), lanes)]
    grad_scale = 1.0 / (samples * STUDENT_TEMP)
    exp_scale = grad_scale / exp_total
    target_scale = grad_scale * target_scale

    mine = us[pl.ds(pl.multiple_of(s * width, width), width), :]

    def gcopy(i):
        part = pl.ds(i * kb, kb)
        return pltpu.make_async_copy(gw.at[part], gw_hbm.at[part], gw_sem.at[i])

    def grad_block(i, acc):
        part = pl.ds(pl.multiple_of(i * kb, kb), kb)
        lg = (expo[part, :] * exp_scale - kern[part, :] * target_scale).astype(BF16)
        lgbuf[...] = lg
        gw[part, :] = lax.dot_general(lg, mine, (((1,), (1,)), ((), ())), preferred_element_type=F32)
        gcopy(i).start()
        local = lgbuf[:, pl.ds(pl.multiple_of(s * lanes, lanes), lanes)]
        return acc + lax.dot_general(local, ws[part, :], (((0,), (0,)), ((), ())), preferred_element_type=F32)

    unit = lax.fori_loop(0, blocks, grad_block, jnp.zeros((lanes, depth), F32)).T
    _, feats = halves(fbuf[s])
    isend[...] = jnp.sum(feats * unit, axis=0, keepdims=True)
    usend[...] = unit.reshape(n_proto, rows, lanes).astype(BF16)

    def unit_copy(i, q, slot):
        return pltpu.make_async_remote_copy(
            src_ref=usend.at[q], dst_ref=ubuf.at[slot], send_sem=u_send.at[i], recv_sem=u_recv.at[slot],
            device_id=(s, q), device_id_type=MESH,
        )

    def inner_copy(i, q, slot):
        return pltpu.make_async_remote_copy(
            src_ref=isend, dst_ref=ibuf.at[slot], send_sem=i_send.at[i], recv_sem=i_recv.at[slot],
            device_id=(s, q), device_id_type=MESH,
        )

    def send_unit(i):
        q = (p + 1 + i) % n_proto
        unit_copy(i, q, p).start()
        inner_copy(i, q, p).start()

    loop(n_proto - 1, send_unit)
    ubuf[p] = usend[p]
    ibuf[p] = isend[...]

    def take_unit(i):
        q = (p + 1 + i) % n_proto
        unit_copy(i, q, q).wait_recv()
        inner_copy(i, q, q).wait_recv()

    loop(n_proto - 1, take_unit)
    unit_grad = jnp.sum(ubuf[...].astype(F32), axis=0)
    inner = jnp.sum(ibuf[...], axis=0)
    scale = sscale[:, pl.ds(pl.multiple_of(s * lanes, lanes), lanes)]
    own_feats = feat_ref[...].astype(F32)[rows:]
    gfeat_ref[...] = scale * unit_grad - (scale * scale * scale * inner) * own_feats

    loop(blocks, lambda i: gcopy(i).wait())
    loop(pairs - 1, lambda i: to_proto(i).wait_send())
    for j in range(n_smp - 1):
        loop(pairs, lambda i, j=j: to_smp(i, j).wait_send())
    for j in range(n_smp):
        loop(pairs, lambda i, j=j: to_core(j, i).wait_send())
    for r in range(iters):
        loop(n_proto - 1, lambda i, r=r: share(r)(i).wait_send())

    def unit_done(i):
        q = (p + 1 + i) % n_proto
        unit_copy(i, q, p).wait_send()
        inner_copy(i, q, p).wait_send()

    loop(n_proto - 1, unit_done)


ITERS = 3


def on_device(n_smp, n_proto, teacher_features, student_features, teacher_weight, student_weight):
    lanes, rows = teacher_features.shape
    protos, depth = teacher_weight.shape
    samples = lanes * n_smp
    width = depth // n_smp
    kb = min(512, protos)
    blocks = protos // kb
    pairs = n_proto // 2
    dma = pltpu.SemaphoreType.DMA
    feats = jnp.concatenate([teacher_features.T, student_features.T], axis=0)
    any_space = pl.BlockSpec(memory_space=pl.ANY)
    vmem = pl.BlockSpec(memory_space=pltpu.VMEM)
    loss, gfeat, gweight = pl.pallas_call(
        functools.partial(kernel, n_smp, n_proto, ITERS, kb),
        out_shape=(
            jax.ShapeDtypeStruct((1, lanes), F32),
            jax.ShapeDtypeStruct((rows, lanes), F32),
            jax.ShapeDtypeStruct((protos, width), F32),
        ),
        in_specs=[vmem, any_space, any_space],
        out_specs=(vmem, vmem, any_space),
        scratch_shapes=[
            pltpu.VMEM((n_smp, n_proto, 2 * rows, lanes), BF16),
            pltpu.VMEM((protos, depth), BF16),
            pltpu.VMEM((protos, depth), BF16),
            pltpu.VMEM((protos, samples), F32),
            pltpu.VMEM((protos, samples), F32),
            pltpu.VMEM((protos, samples), F32),
            pltpu.VMEM((protos, width), F32),
            pltpu.VMEM((depth, samples), BF16),
            pltpu.VMEM((depth, samples), BF16),
            pltpu.VMEM((kb, samples), BF16),
            pltpu.VMEM((1, samples), F32),
            pltpu.VMEM((ITERS, n_proto, 2, samples), F32),
            pltpu.VMEM((1, samples), F32),
            pltpu.VMEM((n_proto, rows, lanes), BF16),
            pltpu.VMEM((n_proto, 1, lanes), F32),
            pltpu.VMEM((n_proto, rows, lanes), BF16),
            pltpu.VMEM((1, lanes), F32),
            dma((blocks,)), dma((blocks,)), dma((blocks,)), dma,
            dma((pairs - 1,)), dma((pairs, n_smp - 1)), dma((n_smp, pairs)), dma((n_smp, n_proto)),
            dma((ITERS, n_proto - 1)), dma((ITERS, n_proto)),
            dma((n_proto - 1,)), dma((n_proto,)), dma((n_proto - 1,)), dma((n_proto,)),
        ],
        compiler_params=pltpu.CompilerParams(
            collective_id=0, has_side_effects=True, vmem_limit_bytes=64000000
        ),
    )(feats, teacher_weight, student_weight)
    return loss[0], gfeat.T, gweight


def solution(mesh):
    placed = (P("smp", "proto"), P("smp", "proto"), P("proto", None), P("proto", None))
    return jax.shard_map(
        functools.partial(on_device, mesh.shape["smp"], mesh.shape["proto"]),
        mesh=mesh,
        in_specs=placed,
        out_specs=(P("smp"), P("smp", "proto"), P("proto", "smp")),
        check_vma=False,
    )
```

```python
import functools

import jax
import jax.numpy as jnp
from jax import lax
from jax.experimental import pallas as pl
from jax.experimental.pallas import tpu as pltpu
from jax.sharding import PartitionSpec as P

TEACHER_TEMP = 0.07
STUDENT_TEMP = 0.1
MESH = pl.DeviceIdType.MESH
F32 = jnp.float32
BF16 = jnp.bfloat16


def loop(count, body):
    if count <= 16:
        for i in range(count):
            body(i)
    else:
        lax.fori_loop(0, count, lambda i, c: (body(i), c)[1], 0)


def fold(x):
    return jnp.sum(x.reshape(x.shape[0] // 8, 8, x.shape[1]), axis=0)


def kernel(
    n_smp, n_proto, iters, kb, ku,
    tfeat_ref, sfeat_ref, wt_hbm, ws_hbm,
    loss_ref, gfeat_ref, mine_ref, lg_ref,
    tbuf, sbuf, wt, ws, kern, logit, expo, ut, us, sscale, rowbuf, stage,
    ubuf, ibuf, usend, isend,
    wt_sem, ws_sem, own_sem, fs_proto, fs_smp, fs_core, fr, sf_send, sf_recv,
    ar_send, ar_recv, u_send, u_recv, i_send, i_recv,
):
    s = lax.axis_index("smp")
    p = lax.axis_index("proto")
    protos_local, depth = wt.shape
    rows, lanes = tfeat_ref.shape
    samples = n_smp * lanes
    protos = n_proto * protos_local
    blocks = protos_local // kb
    pairs = n_proto // 2
    core = p % 2
    pair = p // 2
    mate = pair * 2 + (1 - core)
    width = mine_ref.shape[0]
    my_lanes = pl.ds(pl.multiple_of(s * lanes, lanes), lanes)

    def wcopy(hbm, vmem, sem, i):
        part = pl.ds(i * kb, kb)
        return pltpu.make_async_copy(hbm.at[part], vmem.at[part], sem.at[i])

    own = pltpu.make_async_copy(tfeat_ref, tbuf.at[s, p], own_sem.at[0])
    own_student = pltpu.make_async_copy(sfeat_ref, sbuf.at[s, p], own_sem.at[1])
    own.start()
    own_student.start()
    loop(blocks, lambda i: wcopy(wt_hbm, wt, wt_sem, i).start())
    loop(blocks, lambda i: wcopy(ws_hbm, ws, ws_sem, i).start())

    barrier = pltpu.get_barrier_semaphore()

    def others(body):
        loop(n_proto - 1, lambda i: body(0, i + 1))
        for j in range(1, n_smp):
            loop(n_proto, lambda i, j=j: body(j, i))

    def other(j, i):
        return (s + j) % n_smp, (p + i) % n_proto

    others(lambda j, i: pl.semaphore_signal(barrier, inc=1, device_id=other(j, i), device_id_type=MESH))
    pl.semaphore_wait(barrier, n_smp * n_proto - 1)

    own.wait()
    own_student.wait()

    def chunk(cs, cp, send_sem, target):
        slot = tbuf.at[cs, cp]
        return pltpu.make_async_remote_copy(
            src_ref=slot, dst_ref=slot, send_sem=send_sem, recv_sem=fr.at[cs, cp],
            device_id=target, device_id_type=MESH,
        )

    def peer(i):
        return ((pair + i) % pairs) * 2 + core

    def to_proto(i):
        return chunk(s, p, fs_proto.at[i], (s, peer(i + 1)))

    def to_smp(i, j):
        return chunk(s, peer(i), fs_smp.at[i, j], ((s + 1 + j) % n_smp, p))

    def to_core(j, i):
        return chunk((s + j) % n_smp, peer(i), fs_core.at[j, i], (s, mate))

    def arrived(cs, cp):
        chunk(cs, cp, own_sem.at[0], (s, mate)).wait_recv()

    loop(n_smp - 1, lambda j: to_smp(0, j).start())
    loop(pairs - 1, lambda i: to_proto(i).start())
    to_core(0, 0).start()

    def relay_proto(i):
        arrived(s, peer(i + 1))
        loop(n_smp - 1, lambda j: to_smp(i + 1, j).start())
        to_core(0, i + 1).start()

    loop(pairs - 1, relay_proto)

    def relay_smp(m):
        j = 1 + m // pairs
        i = m % pairs
        arrived((s + j) % n_smp, peer(i))
        to_core(j, i).start()

    loop((n_smp - 1) * pairs, relay_smp)

    def student_copy(j, i, slot):
        return pltpu.make_async_remote_copy(
            src_ref=sbuf.at[s, p], dst_ref=sbuf.at[slot[0], slot[1]], send_sem=sf_send.at[j, i],
            recv_sem=sf_recv.at[slot[0], slot[1]], device_id=other(j, i), device_id_type=MESH,
        )

    others(lambda j, i: student_copy(j, i, (s, p)).start())

    def from_core(m):
        arrived((s + m // pairs) % n_smp, ((pair + m % pairs) % pairs) * 2 + 1 - core)

    loop(n_smp * pairs, from_core)

    def unit_rows(buf, q):
        feats = buf[q].astype(F32).reshape(depth, lanes)
        scale = lax.rsqrt(jnp.sum(feats * feats, axis=0, keepdims=True) + 1e-06)
        return (feats * scale).astype(BF16), scale

    for q in range(n_smp):
        ut[:, q * lanes:(q + 1) * lanes] = unit_rows(tbuf, q)[0]

    def share(r):
        def one(i):
            slot = rowbuf.at[r, p]
            return pltpu.make_async_remote_copy(
                src_ref=slot, dst_ref=slot, send_sem=ar_send.at[r, i], recv_sem=ar_recv.at[r, p],
                device_id=(s, (p + 1 + i) % n_proto), device_id_type=MESH,
            )
        return one

    def gathered(r):
        def one(i):
            q = (p + 1 + i) % n_proto
            slot = rowbuf.at[r, q]
            pltpu.make_async_remote_copy(
                src_ref=slot, dst_ref=slot, send_sem=ar_send.at[r, i], recv_sem=ar_recv.at[r, q],
                device_id=(s, q), device_id_type=MESH,
            ).wait_recv()
        loop(n_proto - 1, one)
        return jnp.sum(rowbuf[r], axis=0)

    def put(r, first, second):
        rowbuf[r, p, 0:1, :] = jnp.sum(first, axis=0, keepdims=True)
        rowbuf[r, p, 1:2, :] = jnp.sum(second, axis=0, keepdims=True)
        loop(n_proto - 1, lambda i: share(r)(i).start())

    zero = jnp.zeros((8, samples), F32)

    def teacher_block(i, acc):
        wcopy(wt_hbm, wt, wt_sem, i).wait()
        part = pl.ds(pl.multiple_of(i * kb, kb), kb)
        value = jnp.exp(jnp.dot(wt[part, :], ut[...], preferred_element_type=F32) * (1.0 / TEACHER_TEMP))
        kern[part, :] = value
        row = 1.0 / jnp.sum(value, axis=1, keepdims=True)
        return acc + fold(value * row)

    def student_block(i, acc):
        wcopy(ws_hbm, ws, ws_sem, i).wait()
        part = pl.ds(pl.multiple_of(i * kb, kb), kb)
        value = jnp.dot(ws[part, :], us[...], preferred_element_type=F32) * (1.0 / STUDENT_TEMP)
        logit[part, :] = value
        value = jnp.exp(value)
        expo[part, :] = value
        return acc + fold(value)

    def unit_sum(ref):
        def block(i, acc):
            part = pl.ds(pl.multiple_of(i * ku, ku), ku)
            local = ref[part, my_lanes].astype(BF16)
            return acc + lax.dot_general(local, ws[part, :], (((0,), (0,)), ((), ())), preferred_element_type=F32)
        return lax.fori_loop(0, protos_local // ku, block, jnp.zeros((lanes, depth), F32)).T

    put(0, lax.fori_loop(0, blocks, teacher_block, zero) * (1.0 / protos), zero)

    others(lambda j, i: student_copy(j, i, other(j, i)).wait_recv())
    for q in range(n_smp):
        here = slice(q * lanes, (q + 1) * lanes)
        us[:, here], sscale[:, here] = unit_rows(sbuf, q)
    mine_ref[...] = us[pl.ds(pl.multiple_of(s * width, width), width), :]

    exp_part = lax.fori_loop(0, blocks, student_block, zero)
    exp_total = None
    exp_unit = None
    for step in range(1, iters):
        total = gathered(step - 1)
        if step == 2:
            exp_total = total[1:2]
        col = protos * (1.0 / (samples * total[0:1]))
        last = step == iters - 1

        def pass_block(i, acc, col=col, last=last):
            part = pl.ds(pl.multiple_of(i * kb, kb), kb)
            value = kern[part, :]
            row = 1.0 / jnp.sum(value * col, axis=1, keepdims=True)
            value = value * row
            if not last:
                return (acc[0] + fold(value),)
            kern[part, :] = value
            return (acc[0] + fold(value), acc[1] + fold(value * logit[part, :]))

        if last:
            first, second = lax.fori_loop(0, blocks, pass_block, (zero, zero))
        else:
            first, second = lax.fori_loop(0, blocks, pass_block, (zero,))[0], exp_part
        put(step, first, second)
        if step == 1:
            exp_unit = unit_sum(expo)

    target_unit = unit_sum(kern)
    total = gathered(iters - 1)
    target_scale = samples * (1.0 / (samples * total[0:1]))
    grad_scale = 1.0 / (samples * STUDENT_TEMP)
    exp_scale = grad_scale / exp_total
    stage[0:1, :] = jnp.log(exp_total) - target_scale * total[1:2]
    target_scale = grad_scale * target_scale
    stage[1:2, :] = exp_scale
    stage[2:3, :] = target_scale
    loss_ref[...] = stage[0:1, my_lanes]

    unit = exp_unit * stage[1:2, my_lanes] - target_unit * stage[2:3, my_lanes]
    feats = sbuf[s].astype(F32).reshape(depth, lanes)
    isend[...] = jnp.sum(feats * unit, axis=0, keepdims=True)
    usend[...] = unit.reshape(n_proto, rows, lanes).astype(BF16)

    def unit_copy(i, q, slot):
        return pltpu.make_async_remote_copy(
            src_ref=usend.at[q], dst_ref=ubuf.at[slot], send_sem=u_send.at[i], recv_sem=u_recv.at[slot],
            device_id=(s, q), device_id_type=MESH,
        )

    def inner_copy(i, q, slot):
        return pltpu.make_async_remote_copy(
            src_ref=isend, dst_ref=ibuf.at[slot], send_sem=i_send.at[i], recv_sem=i_recv.at[slot],
            device_id=(s, q), device_id_type=MESH,
        )

    def send_unit(i):
        q = (p + 1 + i) % n_proto
        unit_copy(i, q, p).start()
        inner_copy(i, q, p).start()

    loop(n_proto - 1, send_unit)

    def grad_block(i, carry):
        part = pl.ds(pl.multiple_of(i * kb, kb), kb)
        lg_ref[part, :] = (expo[part, :] * exp_scale - kern[part, :] * target_scale).astype(BF16)
        return carry

    lax.fori_loop(0, blocks, grad_block, 0)
    ubuf[p] = usend[p]
    ibuf[p] = isend[...]

    def take_unit(i):
        q = (p + 1 + i) % n_proto
        unit_copy(i, q, q).wait_recv()
        inner_copy(i, q, q).wait_recv()

    loop(n_proto - 1, take_unit)
    unit_grad = jnp.sum(ubuf[...].astype(F32), axis=0)
    inner = jnp.sum(ibuf[...], axis=0)
    scale = sscale[:, my_lanes]
    own_feats = sfeat_ref[...].astype(F32)
    gfeat_ref[...] = scale * unit_grad - (scale * scale * scale * inner) * own_feats

    loop(pairs - 1, lambda i: to_proto(i).wait_send())
    for j in range(n_smp - 1):
        loop(pairs, lambda i, j=j: to_smp(i, j).wait_send())
    for j in range(n_smp):
        loop(pairs, lambda i, j=j: to_core(j, i).wait_send())
    others(lambda j, i: student_copy(j, i, (s, p)).wait_send())
    for r in range(iters):
        loop(n_proto - 1, lambda i, r=r: share(r)(i).wait_send())

    def unit_done(i):
        q = (p + 1 + i) % n_proto
        unit_copy(i, q, p).wait_send()
        inner_copy(i, q, p).wait_send()

    loop(n_proto - 1, unit_done)


def finish(lg_ref, mine_ref, loss_ref, gfeat_ref, gw_ref, loss_out, gfeat_out):
    kb = gw_ref.shape[0]
    step = pl.program_id(0)
    lg = lg_ref[pl.ds(pl.multiple_of(step * kb, kb), kb), :]
    gw_ref[...] = lax.dot_general(lg, mine_ref[...], (((1,), (1,)), ((), ())), preferred_element_type=F32)

    @pl.when(step == 0)
    def _():
        loss_out[...] = loss_ref[...]
        gfeat_out[...] = gfeat_ref[...]


ITERS = 3


def on_device(n_smp, n_proto, teacher_features, student_features, teacher_weight, student_weight):
    lanes, rows = teacher_features.shape
    protos, depth = teacher_weight.shape
    samples = lanes * n_smp
    width = depth // n_smp
    kb = min(512, protos)
    ku = min(2048, protos)
    blocks = protos // kb
    pairs = n_proto // 2
    dma = pltpu.SemaphoreType.DMA
    any_space = pl.BlockSpec(memory_space=pl.ANY)
    vmem = pl.BlockSpec(memory_space=pltpu.VMEM)
    loss, gfeat, mine, lg = pl.pallas_call(
        functools.partial(kernel, n_smp, n_proto, ITERS, kb, ku),
        out_shape=(
            jax.ShapeDtypeStruct((1, lanes), F32),
            jax.ShapeDtypeStruct((rows, lanes), F32),
            jax.ShapeDtypeStruct((width, samples), BF16),
            pltpu.VMEM((protos, samples), BF16),
        ),
        in_specs=[vmem, vmem, any_space, any_space],
        out_specs=(vmem, vmem, vmem, vmem),
        scratch_shapes=[
            pltpu.VMEM((n_smp, n_proto, rows, lanes), BF16),
            pltpu.VMEM((n_smp, n_proto, rows, lanes), BF16),
            pltpu.VMEM((protos, depth), BF16),
            pltpu.VMEM((protos, depth), BF16),
            pltpu.VMEM((protos, samples), F32),
            pltpu.VMEM((protos, samples), F32),
            pltpu.VMEM((protos, samples), F32),
            pltpu.VMEM((depth, samples), BF16),
            pltpu.VMEM((depth, samples), BF16),
            pltpu.VMEM((1, samples), F32),
            pltpu.VMEM((ITERS, n_proto, 2, samples), F32),
            pltpu.VMEM((8, samples), F32),
            pltpu.VMEM((n_proto, rows, lanes), BF16),
            pltpu.VMEM((n_proto, 1, lanes), F32),
            pltpu.VMEM((n_proto, rows, lanes), BF16),
            pltpu.VMEM((1, lanes), F32),
            dma((blocks,)), dma((blocks,)), dma((2,)),
            dma((pairs - 1,)), dma((pairs, n_smp - 1)), dma((n_smp, pairs)), dma((n_smp, n_proto)),
            dma((n_smp, n_proto)), dma((n_smp, n_proto)),
            dma((ITERS, n_proto - 1)), dma((ITERS, n_proto)),
            dma((n_proto - 1,)), dma((n_proto,)), dma((n_proto - 1,)), dma((n_proto,)),
        ],
        compiler_params=pltpu.CompilerParams(
            collective_id=0, has_side_effects=True, vmem_limit_bytes=48 * 1024 * 1024
        ),
    )(teacher_features.T, student_features.T, teacher_weight, student_weight)
    gb = min(512, protos)
    whole = lambda shape: pl.BlockSpec(shape, lambda i: (0, 0))
    gweight, loss, gfeat = pl.pallas_call(
        finish,
        grid=(protos // gb,),
        out_shape=(
            jax.ShapeDtypeStruct((protos, width), F32),
            jax.ShapeDtypeStruct((1, lanes), F32),
            jax.ShapeDtypeStruct((rows, lanes), F32),
        ),
        in_specs=[pl.BlockSpec(memory_space=pltpu.VMEM), whole((width, samples)), whole((1, lanes)), whole((rows, lanes))],
        out_specs=(pl.BlockSpec((gb, width), lambda i: (i, 0)), whole((1, lanes)), whole((rows, lanes))),
        compiler_params=pltpu.CompilerParams(vmem_limit_bytes=16 * 1024 * 1024),
    )(lg, mine, loss, gfeat)
    return loss[0], gfeat.T, gweight


def solution(mesh):
    placed = (P("smp", "proto"), P("smp", "proto"), P("proto", None), P("proto", None))
    return jax.shard_map(
        functools.partial(on_device, mesh.shape["smp"], mesh.shape["proto"]),
        mesh=mesh,
        in_specs=placed,
        out_specs=(P("smp"), P("smp", "proto"), P("proto", "smp")),
        check_vma=False,
    )
```

```python
import functools

import jax
import jax.numpy as jnp
from jax import lax
from jax.experimental import pallas as pl
from jax.experimental.pallas import tpu as pltpu
from jax.sharding import PartitionSpec as P

TEACHER_TEMP = 0.07
STUDENT_TEMP = 0.1
MESH = pl.DeviceIdType.MESH
F32 = jnp.float32
BF16 = jnp.bfloat16


def loop(count, body):
    if count <= 16:
        for i in range(count):
            body(i)
    else:
        lax.fori_loop(0, count, lambda i, c: (body(i), c)[1], 0)


def fold(x):
    return jnp.sum(x.reshape(x.shape[0] // 8, 8, x.shape[1]), axis=0)


def kernel(
    n_smp, n_proto, iters, kb, ku,
    tfeat_ref, sfeat_ref, wt_hbm, ws_hbm,
    loss_ref, gfeat_ref, gw_ref,
    tbuf, sbuf, wt, ws, kern, logit, expo, ut, us, sscale, rowbuf, stage,
    ubuf, ibuf, usend, isend,
    wt_sem, ws_sem, own_sem, fs_proto, fs_smp, fs_core, fr, sf_send, sf_recv,
    ar_send, ar_recv, u_send, u_recv, i_send, i_recv,
):
    s = lax.axis_index("smp")
    p = lax.axis_index("proto")
    protos_local, depth = wt.shape
    rows, lanes = tfeat_ref.shape
    samples = n_smp * lanes
    protos = n_proto * protos_local
    blocks = protos_local // kb
    pairs = n_proto // 2
    core = p % 2
    pair = p // 2
    mate = pair * 2 + (1 - core)
    width = gw_ref.shape[1]
    my_lanes = pl.ds(pl.multiple_of(s * lanes, lanes), lanes)

    def wcopy(hbm, vmem, sem, i):
        part = pl.ds(i * kb, kb)
        return pltpu.make_async_copy(hbm.at[part], vmem.at[part], sem.at[i])

    own = pltpu.make_async_copy(tfeat_ref, tbuf.at[s, p], own_sem.at[0])
    own_student = pltpu.make_async_copy(sfeat_ref, sbuf.at[s, p], own_sem.at[1])
    own.start()
    own_student.start()
    loop(blocks, lambda i: wcopy(wt_hbm, wt, wt_sem, i).start())
    loop(blocks, lambda i: wcopy(ws_hbm, ws, ws_sem, i).start())

    barrier = pltpu.get_barrier_semaphore()

    def others(body):
        loop(n_proto - 1, lambda i: body(0, i + 1))
        for j in range(1, n_smp):
            loop(n_proto, lambda i, j=j: body(j, i))

    def other(j, i):
        return (s + j) % n_smp, (p + i) % n_proto

    others(lambda j, i: pl.semaphore_signal(barrier, inc=1, device_id=other(j, i), device_id_type=MESH))
    pl.semaphore_wait(barrier, n_smp * n_proto - 1)

    own.wait()
    own_student.wait()

    def chunk(cs, cp, send_sem, target):
        slot = tbuf.at[cs, cp]
        return pltpu.make_async_remote_copy(
            src_ref=slot, dst_ref=slot, send_sem=send_sem, recv_sem=fr.at[cs, cp],
            device_id=target, device_id_type=MESH,
        )

    def peer(i):
        return ((pair + i) % pairs) * 2 + core

    def to_proto(i):
        return chunk(s, p, fs_proto.at[i], (s, peer(i + 1)))

    def to_smp(i, j):
        return chunk(s, peer(i), fs_smp.at[i, j], ((s + 1 + j) % n_smp, p))

    def to_core(j, i):
        return chunk((s + j) % n_smp, peer(i), fs_core.at[j, i], (s, mate))

    def arrived(cs, cp):
        chunk(cs, cp, own_sem.at[0], (s, mate)).wait_recv()

    loop(n_smp - 1, lambda j: to_smp(0, j).start())
    loop(pairs - 1, lambda i: to_proto(i).start())
    to_core(0, 0).start()

    def relay_proto(i):
        arrived(s, peer(i + 1))
        loop(n_smp - 1, lambda j: to_smp(i + 1, j).start())
        to_core(0, i + 1).start()

    loop(pairs - 1, relay_proto)

    def relay_smp(m):
        j = 1 + m // pairs
        i = m % pairs
        arrived((s + j) % n_smp, peer(i))
        to_core(j, i).start()

    loop((n_smp - 1) * pairs, relay_smp)

    def student_copy(j, i, slot):
        return pltpu.make_async_remote_copy(
            src_ref=sbuf.at[s, p], dst_ref=sbuf.at[slot[0], slot[1]], send_sem=sf_send.at[j, i],
            recv_sem=sf_recv.at[slot[0], slot[1]], device_id=other(j, i), device_id_type=MESH,
        )

    others(lambda j, i: student_copy(j, i, (s, p)).start())

    def from_core(m):
        arrived((s + m // pairs) % n_smp, ((pair + m % pairs) % pairs) * 2 + 1 - core)

    loop(n_smp * pairs, from_core)

    def unit_rows(buf, q):
        feats = buf[q].astype(F32).reshape(depth, lanes)
        scale = lax.rsqrt(jnp.sum(feats * feats, axis=0, keepdims=True) + 1e-06)
        return (feats * scale).astype(BF16), scale

    for q in range(n_smp):
        ut[:, q * lanes:(q + 1) * lanes] = unit_rows(tbuf, q)[0]

    def share(r):
        def one(i):
            slot = rowbuf.at[r, p]
            return pltpu.make_async_remote_copy(
                src_ref=slot, dst_ref=slot, send_sem=ar_send.at[r, i], recv_sem=ar_recv.at[r, p],
                device_id=(s, (p + 1 + i) % n_proto), device_id_type=MESH,
            )
        return one

    def gathered(r):
        def one(i):
            q = (p + 1 + i) % n_proto
            slot = rowbuf.at[r, q]
            pltpu.make_async_remote_copy(
                src_ref=slot, dst_ref=slot, send_sem=ar_send.at[r, i], recv_sem=ar_recv.at[r, q],
                device_id=(s, q), device_id_type=MESH,
            ).wait_recv()
        loop(n_proto - 1, one)
        return jnp.sum(rowbuf[r], axis=0)

    def put(r, first, second):
        rowbuf[r, p, 0:1, :] = jnp.sum(first, axis=0, keepdims=True)
        rowbuf[r, p, 1:2, :] = jnp.sum(second, axis=0, keepdims=True)
        loop(n_proto - 1, lambda i: share(r)(i).start())

    zero = jnp.zeros((8, samples), F32)

    def teacher_block(i, acc):
        wcopy(wt_hbm, wt, wt_sem, i).wait()
        part = pl.ds(pl.multiple_of(i * kb, kb), kb)
        value = jnp.exp(jnp.dot(wt[part, :], ut[...], preferred_element_type=F32) * (1.0 / TEACHER_TEMP))
        kern[part, :] = value
        row = 1.0 / jnp.sum(value, axis=1, keepdims=True)
        return acc + fold(value * row)

    def student_block(i, acc):
        wcopy(ws_hbm, ws, ws_sem, i).wait()
        part = pl.ds(pl.multiple_of(i * kb, kb), kb)
        value = jnp.dot(ws[part, :], us[...], preferred_element_type=F32) * (1.0 / STUDENT_TEMP)
        logit[part, :] = value
        value = jnp.exp(value)
        expo[part, :] = value
        return acc + fold(value)

    def unit_sum(ref):
        def block(i, acc):
            part = pl.ds(pl.multiple_of(i * ku, ku), ku)
            local = ref[part, my_lanes].astype(BF16)
            return acc + lax.dot_general(local, ws[part, :], (((0,), (0,)), ((), ())), preferred_element_type=F32)
        return lax.fori_loop(0, protos_local // ku, block, jnp.zeros((lanes, depth), F32)).T

    put(0, lax.fori_loop(0, blocks, teacher_block, zero) * (1.0 / protos), zero)

    others(lambda j, i: student_copy(j, i, other(j, i)).wait_recv())
    for q in range(n_smp):
        here = slice(q * lanes, (q + 1) * lanes)
        us[:, here], sscale[:, here] = unit_rows(sbuf, q)

    exp_part = lax.fori_loop(0, blocks, student_block, zero)
    exp_total = None
    exp_unit = None
    for step in range(1, iters):
        total = gathered(step - 1)
        if step == 2:
            exp_total = total[1:2]
        col = protos * (1.0 / (samples * total[0:1]))
        last = step == iters - 1

        def pass_block(i, acc, col=col, last=last):
            part = pl.ds(pl.multiple_of(i * kb, kb), kb)
            value = kern[part, :]
            row = 1.0 / jnp.sum(value * col, axis=1, keepdims=True)
            value = value * row
            if not last:
                return (acc[0] + fold(value),)
            kern[part, :] = value
            return (acc[0] + fold(value), acc[1] + fold(value * logit[part, :]))

        if last:
            first, second = lax.fori_loop(0, blocks, pass_block, (zero, zero))
        else:
            first, second = lax.fori_loop(0, blocks, pass_block, (zero,))[0], exp_part
        put(step, first, second)
        if step == 1:
            exp_unit = unit_sum(expo)

    target_unit = unit_sum(kern)
    total = gathered(iters - 1)
    target_scale = samples * (1.0 / (samples * total[0:1]))
    grad_scale = 1.0 / (samples * STUDENT_TEMP)
    exp_scale = grad_scale / exp_total
    stage[0:1, :] = jnp.log(exp_total) - target_scale * total[1:2]
    target_scale = grad_scale * target_scale
    stage[1:2, :] = exp_scale
    stage[2:3, :] = target_scale
    loss_ref[...] = stage[0:1, my_lanes]

    unit = exp_unit * stage[1:2, my_lanes] - target_unit * stage[2:3, my_lanes]
    feats = sbuf[s].astype(F32).reshape(depth, lanes)
    isend[...] = jnp.sum(feats * unit, axis=0, keepdims=True)
    usend[...] = unit.reshape(n_proto, rows, lanes).astype(BF16)

    def unit_copy(i, q, slot):
        return pltpu.make_async_remote_copy(
            src_ref=usend.at[q], dst_ref=ubuf.at[slot], send_sem=u_send.at[i], recv_sem=u_recv.at[slot],
            device_id=(s, q), device_id_type=MESH,
        )

    def inner_copy(i, q, slot):
        return pltpu.make_async_remote_copy(
            src_ref=isend, dst_ref=ibuf.at[slot], send_sem=i_send.at[i], recv_sem=i_recv.at[slot],
            device_id=(s, q), device_id_type=MESH,
        )

    def send_unit(i):
        q = (p + 1 + i) % n_proto
        unit_copy(i, q, p).start()
        inner_copy(i, q, p).start()

    loop(n_proto - 1, send_unit)

    mine = us[pl.ds(pl.multiple_of(s * width, width), width), :]

    def grad_block(i, carry):
        part = pl.ds(pl.multiple_of(i * kb, kb), kb)
        lg = (expo[part, :] * exp_scale - kern[part, :] * target_scale).astype(BF16)
        gw_ref[part, :] = lax.dot_general(lg, mine, (((1,), (1,)), ((), ())), preferred_element_type=F32)
        return carry

    lax.fori_loop(0, blocks, grad_block, 0)
    ubuf[p] = usend[p]
    ibuf[p] = isend[...]

    def take_unit(i):
        q = (p + 1 + i) % n_proto
        unit_copy(i, q, q).wait_recv()
        inner_copy(i, q, q).wait_recv()

    loop(n_proto - 1, take_unit)
    unit_grad = jnp.sum(ubuf[...].astype(F32), axis=0)
    inner = jnp.sum(ibuf[...], axis=0)
    scale = sscale[:, my_lanes]
    own_feats = sbuf[s, p].astype(F32)
    gfeat_ref[...] = scale * unit_grad - (scale * scale * scale * inner) * own_feats

    loop(pairs - 1, lambda i: to_proto(i).wait_send())
    for j in range(n_smp - 1):
        loop(pairs, lambda i, j=j: to_smp(i, j).wait_send())
    for j in range(n_smp):
        loop(pairs, lambda i, j=j: to_core(j, i).wait_send())
    others(lambda j, i: student_copy(j, i, (s, p)).wait_send())
    for r in range(iters):
        loop(n_proto - 1, lambda i, r=r: share(r)(i).wait_send())

    def unit_done(i):
        q = (p + 1 + i) % n_proto
        unit_copy(i, q, p).wait_send()
        inner_copy(i, q, p).wait_send()

    loop(n_proto - 1, unit_done)


def finish(count, gw_ref, loss_ref, gfeat_ref, gw_out, loss_out, gfeat_out, gw_sem, sem):
    kb = gw_ref.shape[0] // count
    copies = [pltpu.make_async_copy(gw_ref.at[pl.ds(i * kb, kb)], gw_out.at[pl.ds(i * kb, kb)], gw_sem.at[i]) for i in range(count)]
    copies.append(pltpu.make_async_copy(loss_ref, loss_out, sem.at[0]))
    copies.append(pltpu.make_async_copy(gfeat_ref, gfeat_out, sem.at[1]))
    for copy in copies:
        copy.start()
    for copy in copies:
        copy.wait()


ITERS = 3


def on_device(n_smp, n_proto, teacher_features, student_features, teacher_weight, student_weight):
    lanes, rows = teacher_features.shape
    protos, depth = teacher_weight.shape
    samples = lanes * n_smp
    width = depth // n_smp
    kb = min(512, protos)
    ku = min(2048, protos)
    blocks = protos // kb
    pairs = n_proto // 2
    dma = pltpu.SemaphoreType.DMA
    any_space = pl.BlockSpec(memory_space=pl.ANY)
    vmem = pl.BlockSpec(memory_space=pltpu.VMEM)
    hbm = pl.BlockSpec(memory_space=pltpu.HBM)
    loss, gfeat, gweight = pl.pallas_call(
        functools.partial(kernel, n_smp, n_proto, ITERS, kb, ku),
        out_shape=(
            pltpu.VMEM((1, lanes), F32),
            pltpu.VMEM((rows, lanes), F32),
            pltpu.VMEM((protos, width), F32),
        ),
        in_specs=[hbm, hbm, any_space, any_space],
        out_specs=(vmem, vmem, vmem),
        scratch_shapes=[
            pltpu.VMEM((n_smp, n_proto, rows, lanes), BF16),
            pltpu.VMEM((n_smp, n_proto, rows, lanes), BF16),
            pltpu.VMEM((protos, depth), BF16),
            pltpu.VMEM((protos, depth), BF16),
            pltpu.VMEM((protos, samples), F32),
            pltpu.VMEM((protos, samples), F32),
            pltpu.VMEM((protos, samples), F32),
            pltpu.VMEM((depth, samples), BF16),
            pltpu.VMEM((depth, samples), BF16),
            pltpu.VMEM((1, samples), F32),
            pltpu.VMEM((ITERS, n_proto, 2, samples), F32),
            pltpu.VMEM((8, samples), F32),
            pltpu.VMEM((n_proto, rows, lanes), BF16),
            pltpu.VMEM((n_proto, 1, lanes), F32),
            pltpu.VMEM((n_proto, rows, lanes), BF16),
            pltpu.VMEM((1, lanes), F32),
            dma((blocks,)), dma((blocks,)), dma((2,)),
            dma((pairs - 1,)), dma((pairs, n_smp - 1)), dma((n_smp, pairs)), dma((n_smp, n_proto)),
            dma((n_smp, n_proto)), dma((n_smp, n_proto)),
            dma((ITERS, n_proto - 1)), dma((ITERS, n_proto)),
            dma((n_proto - 1,)), dma((n_proto,)), dma((n_proto - 1,)), dma((n_proto,)),
        ],
        compiler_params=pltpu.CompilerParams(
            collective_id=0, has_side_effects=True, vmem_limit_bytes=48 * 1024 * 1024
        ),
    )(teacher_features.T, student_features.T, teacher_weight, student_weight)
    gweight, loss, gfeat = pl.pallas_call(
        functools.partial(finish, 8),
        out_shape=(
            jax.ShapeDtypeStruct((protos, width), F32),
            jax.ShapeDtypeStruct((1, lanes), F32),
            jax.ShapeDtypeStruct((rows, lanes), F32),
        ),
        in_specs=[vmem, vmem, vmem],
        out_specs=(hbm, hbm, hbm),
        scratch_shapes=[dma((8,)), dma((2,))],
        compiler_params=pltpu.CompilerParams(vmem_limit_bytes=1024 * 1024),
    )(gweight, loss, gfeat)
    return loss[0], gfeat.T, gweight


def solution(mesh):
    placed = (P("smp", "proto"), P("smp", "proto"), P("proto", None), P("proto", None))
    return jax.shard_map(
        functools.partial(on_device, mesh.shape["smp"], mesh.shape["proto"]),
        mesh=mesh,
        in_specs=placed,
        out_specs=(P("smp"), P("smp", "proto"), P("proto", "smp")),
        check_vma=False,
    )
```

```python
import functools

import jax
import jax.numpy as jnp
from jax import lax
from jax.experimental import pallas as pl
from jax.experimental.pallas import tpu as pltpu
from jax.sharding import PartitionSpec as P

TEACHER_TEMP = 0.07
STUDENT_TEMP = 0.1
MESH = pl.DeviceIdType.MESH
F32 = jnp.float32
BF16 = jnp.bfloat16


def loop(count, body):
    if count <= 16:
        for i in range(count):
            body(i)
    else:
        lax.fori_loop(0, count, lambda i, c: (body(i), c)[1], 0)


def fold(x):
    return jnp.sum(x.reshape(x.shape[0] // 8, 8, x.shape[1]), axis=0)


def kernel(
    n_smp, n_proto, iters, kb, ku,
    tfeat_ref, sfeat_ref, wt_hbm, ws_hbm,
    loss_ref, gfeat_ref, gw_ref,
    tbuf, sbuf, wt, ws, kern, logit, expo, ut, us, sscale, rowbuf, stage,
    ubuf, ibuf, usend, isend,
    wt_sem, ws_sem, own_sem, fs_proto, fs_smp, fs_core, fr, sf_send, sf_recv,
    ar_send, ar_recv, u_send, u_recv, i_send, i_recv,
):
    s = lax.axis_index("smp")
    p = lax.axis_index("proto")
    protos_local, depth = wt.shape
    rows, lanes = tfeat_ref.shape
    samples = n_smp * lanes
    protos = n_proto * protos_local
    blocks = protos_local // kb
    pairs = n_proto // 2
    core = p % 2
    pair = p // 2
    mate = pair * 2 + (1 - core)
    width = gw_ref.shape[1]
    my_lanes = pl.ds(pl.multiple_of(s * lanes, lanes), lanes)

    def wcopy(hbm, vmem, sem, i):
        part = pl.ds(i * kb, kb)
        return pltpu.make_async_copy(hbm.at[part], vmem.at[part], sem.at[i])

    own = pltpu.make_async_copy(tfeat_ref, tbuf.at[s, p], own_sem.at[0])
    own_student = pltpu.make_async_copy(sfeat_ref, sbuf.at[s, p], own_sem.at[1])
    own.start()
    own_student.start()
    loop(blocks, lambda i: wcopy(wt_hbm, wt, wt_sem, i).start())
    loop(blocks, lambda i: wcopy(ws_hbm, ws, ws_sem, i).start())

    barrier = pltpu.get_barrier_semaphore()

    def others(body):
        loop(n_proto - 1, lambda i: body(0, i + 1))
        for j in range(1, n_smp):
            loop(n_proto, lambda i, j=j: body(j, i))

    def other(j, i):
        return (s + j) % n_smp, (p + i) % n_proto

    others(lambda j, i: pl.semaphore_signal(barrier, inc=1, device_id=other(j, i), device_id_type=MESH))
    pl.semaphore_wait(barrier, n_smp * n_proto - 1)

    own.wait()
    own_student.wait()

    def chunk(cs, cp, send_sem, target):
        slot = tbuf.at[cs, cp]
        return pltpu.make_async_remote_copy(
            src_ref=slot, dst_ref=slot, send_sem=send_sem, recv_sem=fr.at[cs, cp],
            device_id=target, device_id_type=MESH,
        )

    def peer(i):
        return ((pair + i) % pairs) * 2 + core

    def to_proto(i):
        return chunk(s, p, fs_proto.at[i], (s, peer(i + 1)))

    def to_smp(i, j):
        return chunk(s, peer(i), fs_smp.at[i, j], ((s + 1 + j) % n_smp, p))

    def to_core(j, i):
        return chunk((s + j) % n_smp, peer(i), fs_core.at[j, i], (s, mate))

    def arrived(cs, cp):
        chunk(cs, cp, own_sem.at[0], (s, mate)).wait_recv()

    loop(n_smp - 1, lambda j: to_smp(0, j).start())
    loop(pairs - 1, lambda i: to_proto(i).start())
    to_core(0, 0).start()

    def relay_proto(i):
        arrived(s, peer(i + 1))
        loop(n_smp - 1, lambda j: to_smp(i + 1, j).start())
        to_core(0, i + 1).start()

    loop(pairs - 1, relay_proto)

    def relay_smp(m):
        j = 1 + m // pairs
        i = m % pairs
        arrived((s + j) % n_smp, peer(i))
        to_core(j, i).start()

    loop((n_smp - 1) * pairs, relay_smp)

    def student_copy(j, i, slot):
        return pltpu.make_async_remote_copy(
            src_ref=sbuf.at[s, p], dst_ref=sbuf.at[slot[0], slot[1]], send_sem=sf_send.at[j, i],
            recv_sem=sf_recv.at[slot[0], slot[1]], device_id=other(j, i), device_id_type=MESH,
        )

    others(lambda j, i: student_copy(j, i, (s, p)).start())

    def from_core(m):
        arrived((s + m // pairs) % n_smp, ((pair + m % pairs) % pairs) * 2 + 1 - core)

    loop(n_smp * pairs, from_core)

    def unit_rows(buf, q):
        feats = buf[q].astype(F32).reshape(depth, lanes)
        scale = lax.rsqrt(jnp.sum(feats * feats, axis=0, keepdims=True) + 1e-06)
        return (feats * scale).astype(BF16), scale

    for q in range(n_smp):
        ut[:, q * lanes:(q + 1) * lanes] = unit_rows(tbuf, q)[0]

    def share(r):
        def one(i):
            slot = rowbuf.at[r, p]
            return pltpu.make_async_remote_copy(
                src_ref=slot, dst_ref=slot, send_sem=ar_send.at[r, i], recv_sem=ar_recv.at[r, p],
                device_id=(s, (p + 1 + i) % n_proto), device_id_type=MESH,
            )
        return one

    def gathered(r):
        def one(i):
            q = (p + 1 + i) % n_proto
            slot = rowbuf.at[r, q]
            pltpu.make_async_remote_copy(
                src_ref=slot, dst_ref=slot, send_sem=ar_send.at[r, i], recv_sem=ar_recv.at[r, q],
                device_id=(s, q), device_id_type=MESH,
            ).wait_recv()
        loop(n_proto - 1, one)
        return jnp.sum(rowbuf[r], axis=0)

    def put(r, first, second):
        rowbuf[r, p, 0:1, :] = jnp.sum(first, axis=0, keepdims=True)
        rowbuf[r, p, 1:2, :] = jnp.sum(second, axis=0, keepdims=True)
        loop(n_proto - 1, lambda i: share(r)(i).start())

    zero = jnp.zeros((8, samples), F32)

    def teacher_block(i, acc):
        wcopy(wt_hbm, wt, wt_sem, i).wait()
        part = pl.ds(pl.multiple_of(i * kb, kb), kb)
        value = jnp.exp(jnp.dot(wt[part, :], ut[...], preferred_element_type=F32) * (1.0 / TEACHER_TEMP))
        kern[part, :] = value
        row = 1.0 / jnp.sum(value, axis=1, keepdims=True)
        return acc + fold(value * row)

    def student_block(i, acc):
        wcopy(ws_hbm, ws, ws_sem, i).wait()
        part = pl.ds(pl.multiple_of(i * kb, kb), kb)
        value = jnp.dot(ws[part, :], us[...], preferred_element_type=F32) * (1.0 / STUDENT_TEMP)
        logit[part, :] = value
        value = jnp.exp(value)
        expo[part, :] = value
        return acc + fold(value)

    def unit_sum(ref):
        def block(i, acc):
            part = pl.ds(pl.multiple_of(i * ku, ku), ku)
            local = ref[part, my_lanes].astype(BF16)
            return acc + lax.dot_general(local, ws[part, :], (((0,), (0,)), ((), ())), preferred_element_type=F32)
        return lax.fori_loop(0, protos_local // ku, block, jnp.zeros((lanes, depth), F32)).T

    put(0, lax.fori_loop(0, blocks, teacher_block, zero) * (1.0 / protos), zero)

    others(lambda j, i: student_copy(j, i, other(j, i)).wait_recv())
    for q in range(n_smp):
        here = slice(q * lanes, (q + 1) * lanes)
        us[:, here], sscale[:, here] = unit_rows(sbuf, q)

    exp_part = lax.fori_loop(0, blocks, student_block, zero)
    exp_total = None
    exp_unit = None
    for step in range(1, iters):
        total = gathered(step - 1)
        if step == 2:
            exp_total = total[1:2]
        col = protos * (1.0 / (samples * total[0:1]))
        last = step == iters - 1

        def pass_block(i, acc, col=col, last=last):
            part = pl.ds(pl.multiple_of(i * kb, kb), kb)
            value = kern[part, :]
            row = 1.0 / jnp.sum(value * col, axis=1, keepdims=True)
            value = value * row
            if not last:
                return (acc[0] + fold(value),)
            kern[part, :] = value
            return (acc[0] + fold(value), acc[1] + fold(value * logit[part, :]))

        if last:
            first, second = lax.fori_loop(0, blocks, pass_block, (zero, zero))
        else:
            first, second = lax.fori_loop(0, blocks, pass_block, (zero,))[0], exp_part
        put(step, first, second)
        if step == 1:
            exp_unit = unit_sum(expo)

    target_unit = unit_sum(kern)
    total = gathered(iters - 1)
    target_scale = samples * (1.0 / (samples * total[0:1]))
    grad_scale = 1.0 / (samples * STUDENT_TEMP)
    exp_scale = grad_scale / exp_total
    stage[0:1, :] = jnp.log(exp_total) - target_scale * total[1:2]
    target_scale = grad_scale * target_scale
    stage[1:2, :] = exp_scale
    stage[2:3, :] = target_scale
    loss_ref[...] = stage[0:1, my_lanes]

    unit = exp_unit * stage[1:2, my_lanes] - target_unit * stage[2:3, my_lanes]
    feats = sbuf[s].astype(F32).reshape(depth, lanes)
    isend[...] = jnp.sum(feats * unit, axis=0, keepdims=True)
    usend[...] = unit.reshape(n_proto, rows, lanes).astype(BF16)

    def unit_copy(i, q, slot):
        return pltpu.make_async_remote_copy(
            src_ref=usend.at[q], dst_ref=ubuf.at[slot], send_sem=u_send.at[i], recv_sem=u_recv.at[slot],
            device_id=(s, q), device_id_type=MESH,
        )

    def inner_copy(i, q, slot):
        return pltpu.make_async_remote_copy(
            src_ref=isend, dst_ref=ibuf.at[slot], send_sem=i_send.at[i], recv_sem=i_recv.at[slot],
            device_id=(s, q), device_id_type=MESH,
        )

    def send_unit(i):
        q = (p + 1 + i) % n_proto
        unit_copy(i, q, p).start()
        inner_copy(i, q, p).start()

    loop(n_proto - 1, send_unit)

    mine = us[pl.ds(pl.multiple_of(s * width, width), width), :]

    def grad_block(i, carry):
        part = pl.ds(pl.multiple_of(i * kb, kb), kb)
        lg = (expo[part, :] * exp_scale - kern[part, :] * target_scale).astype(BF16)
        gw_ref[part, :] = lax.dot_general(lg, mine, (((1,), (1,)), ((), ())), preferred_element_type=F32)
        return carry

    lax.fori_loop(0, blocks, grad_block, 0)
    ubuf[p] = usend[p]
    ibuf[p] = isend[...]

    def take_unit(i):
        q = (p + 1 + i) % n_proto
        unit_copy(i, q, q).wait_recv()
        inner_copy(i, q, q).wait_recv()

    loop(n_proto - 1, take_unit)
    unit_grad = jnp.sum(ubuf[...].astype(F32), axis=0)
    inner = jnp.sum(ibuf[...], axis=0)
    scale = sscale[:, my_lanes]
    own_feats = sbuf[s, p].astype(F32)
    gfeat_ref[...] = scale * unit_grad - (scale * scale * scale * inner) * own_feats

    loop(pairs - 1, lambda i: to_proto(i).wait_send())
    for j in range(n_smp - 1):
        loop(pairs, lambda i, j=j: to_smp(i, j).wait_send())
    for j in range(n_smp):
        loop(pairs, lambda i, j=j: to_core(j, i).wait_send())
    others(lambda j, i: student_copy(j, i, (s, p)).wait_send())
    for r in range(iters):
        loop(n_proto - 1, lambda i, r=r: share(r)(i).wait_send())

    def unit_done(i):
        q = (p + 1 + i) % n_proto
        unit_copy(i, q, p).wait_send()
        inner_copy(i, q, p).wait_send()

    loop(n_proto - 1, unit_done)


def finish(count, gw_ref, loss_ref, gfeat_ref, gw_out, loss_out, gfeat_out, gw_sem, sem):
    kb = gw_ref.shape[0] // count
    copies = [pltpu.make_async_copy(gw_ref.at[pl.ds(i * kb, kb)], gw_out.at[pl.ds(i * kb, kb)], gw_sem.at[i]) for i in range(count)]
    copies.append(pltpu.make_async_copy(loss_ref, loss_out, sem.at[0]))
    copies.append(pltpu.make_async_copy(gfeat_ref, gfeat_out, sem.at[1]))
    for copy in copies:
        copy.start()
    for copy in copies:
        copy.wait()


ITERS = 3


def on_device(n_smp, n_proto, teacher_features, student_features, teacher_weight, student_weight):
    lanes, rows = teacher_features.shape
    protos, depth = teacher_weight.shape
    samples = lanes * n_smp
    width = depth // n_smp
    kb = min(4096, protos)
    ku = min(2048, protos)
    blocks = protos // kb
    pairs = n_proto // 2
    dma = pltpu.SemaphoreType.DMA
    any_space = pl.BlockSpec(memory_space=pl.ANY)
    vmem = pl.BlockSpec(memory_space=pltpu.VMEM)
    hbm = pl.BlockSpec(memory_space=pltpu.HBM)
    loss, gfeat, gweight = pl.pallas_call(
        functools.partial(kernel, n_smp, n_proto, ITERS, kb, ku),
        out_shape=(
            pltpu.VMEM((1, lanes), F32),
            pltpu.VMEM((rows, lanes), F32),
            pltpu.VMEM((protos, width), F32),
        ),
        in_specs=[hbm, hbm, any_space, any_space],
        out_specs=(vmem, vmem, vmem),
        scratch_shapes=[
            pltpu.VMEM((n_smp, n_proto, rows, lanes), BF16),
            pltpu.VMEM((n_smp, n_proto, rows, lanes), BF16),
            pltpu.VMEM((protos, depth), BF16),
            pltpu.VMEM((protos, depth), BF16),
            pltpu.VMEM((protos, samples), F32),
            pltpu.VMEM((protos, samples), F32),
            pltpu.VMEM((protos, samples), F32),
            pltpu.VMEM((depth, samples), BF16),
            pltpu.VMEM((depth, samples), BF16),
            pltpu.VMEM((1, samples), F32),
            pltpu.VMEM((ITERS, n_proto, 2, samples), F32),
            pltpu.VMEM((8, samples), F32),
            pltpu.VMEM((n_proto, rows, lanes), BF16),
            pltpu.VMEM((n_proto, 1, lanes), F32),
            pltpu.VMEM((n_proto, rows, lanes), BF16),
            pltpu.VMEM((1, lanes), F32),
            dma((blocks,)), dma((blocks,)), dma((2,)),
            dma((pairs - 1,)), dma((pairs, n_smp - 1)), dma((n_smp, pairs)), dma((n_smp, n_proto)),
            dma((n_smp, n_proto)), dma((n_smp, n_proto)),
            dma((ITERS, n_proto - 1)), dma((ITERS, n_proto)),
            dma((n_proto - 1,)), dma((n_proto,)), dma((n_proto - 1,)), dma((n_proto,)),
        ],
        compiler_params=pltpu.CompilerParams(
            collective_id=0, has_side_effects=True, vmem_limit_bytes=48 * 1024 * 1024
        ),
    )(teacher_features.T, student_features.T, teacher_weight, student_weight)
    gweight, loss, gfeat = pl.pallas_call(
        functools.partial(finish, 8),
        out_shape=(
            jax.ShapeDtypeStruct((protos, width), F32),
            jax.ShapeDtypeStruct((1, lanes), F32),
            jax.ShapeDtypeStruct((rows, lanes), F32),
        ),
        in_specs=[vmem, vmem, vmem],
        out_specs=(hbm, hbm, hbm),
        scratch_shapes=[dma((8,)), dma((2,))],
        compiler_params=pltpu.CompilerParams(vmem_limit_bytes=1024 * 1024),
    )(gweight, loss, gfeat)
    return loss[0], gfeat.T, gweight


def solution(mesh):
    placed = (P("smp", "proto"), P("smp", "proto"), P("proto", None), P("proto", None))
    return jax.shard_map(
        functools.partial(on_device, mesh.shape["smp"], mesh.shape["proto"]),
        mesh=mesh,
        in_specs=placed,
        out_specs=(P("smp"), P("smp", "proto"), P("proto", "smp")),
        check_vma=False,
    )
```
